32 devices in a mesh: groups: 2 (over x), dp: 16 (over z, y, core).
Axes of the slice: x: 2, y: 2, z: 4, core: 2. Of those that a mesh axis runs over, the one named last changes fastest.
Arguments:
- query_rows: bfloat16 [32, 32, 768], P(('groups', 'dp')), parts along dimension 0, may hold values from -6 to 6
- proj_weight: bfloat16 [768, 4096], replicated, may hold values from -0.21875 to 0.21875
- proj_bias: bfloat16 [4096], replicated, may hold values from -3 to 3
- candidates: int32 [32, 2], P(('groups', 'dp')), parts along dimension 0, may hold values from 0 to 15, as said below
- caption_states: bfloat16 [32, 4, 4096], P(('groups', 'dp')), parts along dimension 0, may hold values from -24 to 24
- caption_ids: int32 [32, 4], P(('groups', 'dp')), parts along dimension 0, may hold values from 0 to 32127
- caption_lengths: int32 [32], P(('groups', 'dp')), parts along dimension 0, may hold values from 1 to 4
- norm_gain: float32 [4096], replicated, may hold values from 0.5 to 1.5
- head_weight: bfloat16 [4096, 32128], P(None, 'dp'), may hold values from -0.5 to 0.5
Outputs:
- token_loglik: float32 [32, 2, 4], P(('groups', 'dp')), parts along dimension 0
The draws below stay inside these ranges and needn't reach their ends.
There are 2 independent parts, one for each index of `groups`. The reference program is written for one: setup_inputs(seed, part) draws one part's arguments, and reference() takes and returns one part's arrays. A program takes and returns all parts, laid end to end along the dimension named above; an argument that names none is the same for every part. Nothing has to cross between parts.
Inputs may be any that keep to these rules, and one draw needn't show every extreme that they name: Entry (i, k) names stored caption c, held on data shard c. The candidates of one data shard's images name distinct data shards. Each data shard's captions are named by at most 4 candidates in all, and some data shard's by exactly that many.
All inputs are finite; a program needn't handle non-finite values.
Results may differ from the reference program's by a relative error of at most 0.0006.
Values may be sent and summed in bfloat16 or wider, within the bound.
A program may use at most 128 MiB of HBM per device.

```python
import math
import jax
import jax.numpy as jnp
import numpy as np
from jax import lax

D = 4096
HEAD_DIM = 64
QDIM = 768
PREFIX = 32
VOCAB = 32128
TOPK = 2
CAP_LEN = 4
IMG_DEV = 1
IMAGES = 16
CAP_DEV = 1
CAPTIONS = 16
N_DP = 16


def draw_candidates(key, part):
    devices = N_DP
    per_shard = IMG_DEV * TOPK
    key_order = jax.random.fold_in(key, 11)
    key_shift = jax.random.fold_in(key, 23)
    order = jax.random.permutation(key_order, devices)
    ranks = jnp.arange(devices)
    loads = jnp.where(ranks < devices // 4, 2 * per_shard, jnp.where(ranks < 3 * devices // 4, per_shard, 0))
    starts = jnp.cumsum(loads) - loads
    source = jnp.arange(devices)[:, None]
    within = jnp.arange(per_shard)[None, :]
    slots = within * devices + source
    block_rank = jnp.sum((starts[None, None, :] <= slots[:, :, None]).astype(jnp.int32), -1) - 1
    owners = jnp.take(order, block_rank)
    offset = slots - jnp.take(starts, block_rank)
    shifts = jax.random.randint(key_shift, (devices,), 0, CAP_DEV)
    stored_row = (offset + jnp.take(shifts, owners)) % CAP_DEV
    chosen = owners * CAP_DEV + stored_row
    return chosen.reshape(devices * IMG_DEV, TOPK).astype(jnp.int32)


def draw_caption_states(key, part):
    values = jax.random.normal(jax.random.fold_in(key, 5), (CAPTIONS, CAP_LEN, D), jnp.float32)
    values = jnp.clip(values, -6.0, 6.0)
    return values.astype(jnp.bfloat16)


def draw_head_weight(key, part):
    spread = (9.0 / D) ** 0.5
    limit = min(6.0, 0.5 / spread)
    values = jax.random.normal(jax.random.fold_in(key, 3), (D, VOCAB), jnp.float32)
    values = jnp.clip(values, -limit, limit) * spread
    return values.astype(jnp.bfloat16)


def set_ends(entries, own_key, smallest, high):
    longest = entries.shape.index(max(entries.shape))
    spots = []
    for shift in (0, 1):
        where = [jax.random.randint(jax.random.fold_in(own_key, axis), (), 0, length) for axis, length in enumerate(entries.shape)]
        where[longest] = (where[longest] + shift) % entries.shape[longest]
        spots.append(tuple(where))
    return entries.at[spots[0]].set(smallest).at[spots[1]].set(high)


def block_levels(own_key, shape, shards, smallest, high):
    level = 1.0
    for position, parts in shards:
        draws = jax.random.uniform(jax.random.fold_in(jax.random.fold_in(own_key, 6), position), (parts,), jnp.float32, smallest / len(shards), high / len(shards))
        level = level * jnp.repeat(jnp.exp(draws), shape[position] // parts).reshape((-1,) + (1,) * (len(shape) - 1 - position))
    return level


def rank_table(count, lean):
    weights = [(1 << 20) // math.isqrt(grade ** lean) + 1 for grade in range(1, count + 1)]
    scale = 1 + sum(weights) // (1 << 30)
    return np.cumsum(np.array([max(1, weight // scale) for weight in weights]))


def skewed_ids(own_key, dims, number_of, lean):
    listing = rank_table(number_of, lean)
    pick = jax.random.randint(jax.random.fold_in(own_key, 1), dims, 0, int(listing[number_of - 1]))
    rank = jnp.searchsorted(jnp.asarray(listing, jnp.int32), pick, side="right")
    return jax.random.permutation(jax.random.fold_in(own_key, 2), number_of)[rank].astype(jnp.int32)


def noise(own_key, shape, scale, bound, split=(), held_as=jnp.bfloat16):
    values = scale * jax.random.normal(own_key, shape, jnp.float32)
    if split:
        values = values * block_levels(own_key, shape, split, -0.22, 0.18)
    return jnp.clip(values, -bound, bound).astype(held_as)


def setup_inputs(seed: int = 0, part: int = 0) -> dict:
    streams_of = jax.random.split(jax.random.key(seed), 10)
    part_splits = jax.random.split(jax.random.fold_in(streams_of[9], part), 10)
    return {
        "query_rows": noise(part_splits[0], (IMAGES, PREFIX, QDIM), 1.0, 6.0, ((0, 16),)),
        "proj_weight": noise(streams_of[1], (QDIM, D), QDIM ** -0.5, 0.21875),
        "proj_bias": noise(streams_of[2], (D,), 0.5, 3.0),
        "candidates": draw_candidates(jax.random.fold_in(jax.random.fold_in(streams_of[9], part), 71), part),
        "caption_states": draw_caption_states(jax.random.fold_in(jax.random.fold_in(streams_of[9], part), 71), part),
        "caption_ids": set_ends(skewed_ids(part_splits[5], (CAPTIONS, CAP_LEN), VOCAB, 2), jax.random.fold_in(part_splits[5], 3), 0, VOCAB - 1).astype(jnp.int32),
        "caption_lengths": set_ends(jax.random.randint(part_splits[6], (CAPTIONS,), 1, CAP_LEN + 1), jax.random.fold_in(part_splits[6], 1), 1, CAP_LEN).astype(jnp.int32),
        "norm_gain": jnp.clip(1.0 + 0.1 * jax.random.normal(streams_of[7], (D,), jnp.float32), 0.5, 1.5),
        "head_weight": draw_head_weight(jax.random.fold_in(streams_of[9], 71), part),
    }


score_scale = 0.015625
eps = 1e-06

def project(rows, proj_weight, proj_bias):
    summed = jnp.dot(rows, proj_weight, preferred_element_type=jnp.float32)
    return (summed + proj_bias.astype(jnp.float32)).astype(jnp.bfloat16)

def attend(projected, states, norm_gain):
    prefix_len = projected.shape[0]
    cap_len, width = states.shape
    heads = width // HEAD_DIM
    keys = jnp.concatenate([projected, states], 0)
    query = states.reshape(cap_len, heads, HEAD_DIM).astype(jnp.float32)
    keyed = keys.reshape(prefix_len + cap_len, heads, HEAD_DIM).astype(jnp.float32)
    scores = jnp.einsum('thd,jhd->htj', query, keyed) * score_scale
    key_pos = jnp.arange(prefix_len + cap_len)[None, :]
    tok_pos = jnp.arange(cap_len)[:, None]
    allowed = (key_pos < prefix_len) | (key_pos - prefix_len <= tok_pos)
    scores = jnp.where(allowed[None], scores, -jnp.inf)
    row_max = lax.optimization_barrier(jnp.max(scores, -1, keepdims=True))
    expo = jnp.exp(scores - row_max)
    weights = (expo / lax.optimization_barrier(jnp.sum(expo, -1, keepdims=True))).astype(jnp.bfloat16)
    mixed_out = jnp.einsum('htj,jhd->thd', weights.astype(jnp.float32), keyed).reshape(cap_len, width)
    mixed = states.astype(jnp.float32) + mixed_out
    normed = mixed * lax.rsqrt(lax.optimization_barrier(jnp.mean(mixed * mixed, -1, keepdims=True)) + eps) * norm_gain
    return normed.astype(jnp.bfloat16)

def reference(query_rows, proj_weight, proj_bias, candidates, caption_states, caption_ids, caption_lengths, norm_gain, head_weight):

    def one_image(inputs):
        rows, chosen = inputs
        projected = project(rows, proj_weight, proj_bias)
        states = caption_states[chosen]
        return jax.vmap(lambda one: attend(projected, one, norm_gain))(states)
    hidden_all = lax.map(one_image, (query_rows, candidates))
    token_ids = caption_ids[candidates].reshape(-1)
    lengths = caption_lengths[candidates]
    width = hidden_all.shape[-1]
    row_blocks = hidden_all.reshape(4, -1, width)
    id_blocks = token_ids.reshape(4, -1)

    def score_block(inputs):
        block, block_ids = inputs
        logits = jnp.dot(block, head_weight, preferred_element_type=jnp.float32)
        row_max = lax.optimization_barrier(jnp.max(logits, -1))
        row_sum = lax.optimization_barrier(jnp.sum(jnp.exp(logits - row_max[:, None]), -1))
        picked = jnp.take_along_axis(logits, block_ids[:, None], 1)[:, 0]
        return picked - (row_max + jnp.log(row_sum))
    loglik = lax.map(score_block, (row_blocks, id_blocks)).reshape(lengths.shape + (CAP_LEN,))
    inside = jnp.arange(CAP_LEN)[None, None, :] < lengths[:, :, None]
    return jnp.where(inside, loglik, jnp.float32(0.0))
```

```python
import functools

import jax
import jax.numpy as jnp
from jax import lax
from jax.experimental import pallas as pl
from jax.experimental.pallas import tpu as pltpu
from jax.sharding import PartitionSpec as P

HEAD_DIM = 64
SCALE = 0.015625
EPS = 1e-06
LANES = 128
GROUP = 256
MESH = pl.DeviceIdType.MESH
P_CHUNKS = 4
H_SPLIT = (1, 1, 1, 1)
TILE = 256
PACE = 1.4


def ring_order(count):
    return sorted(range(1, count), key=lambda d: (min(d, count - d), d))


def nearest(a, count):
    if count != 4:
        return [lax.rem(a + d, count) for d in ring_order(count)]
    high = a // 2
    low = 1 - high
    near = high * (3 - a) + low * a
    return [high * (3 - q) + low * q for q in (1 - near, 2, 3)]


def feature_spans(width):
    unit, at, spans = width // sum(H_SPLIT), 0, []
    for share in H_SPLIT:
        spans.append((at, share * unit))
        at += share * unit
    return spans


def kernel(
    n,
    rows_b,
    query_hbm,
    pw_hbm,
    bias_hbm,
    cand_hbm,
    state_hbm,
    ids_hbm,
    len_hbm,
    gain_hbm,
    hw_hbm,
    out_ref,
    query_ref,
    bias_ref,
    cand_ref,
    state_ref,
    ids_ref,
    len_ref,
    gain_ref,
    in_sem,
    pw,
    hw,
    caps,
    kv,
    hid,
    flat,
    logit,
    st_in,
    pw_sem,
    hw_sem,
    s1,
    z1,
    y1,
    c1,
    s2,
    z2,
    y2,
    c2,
    ss3,
    sr3,
):
    B = rows_b
    A = n // (2 * B)
    g = lax.axis_index("groups")
    p = lax.axis_index("dp")
    c = lax.rem(p, 2)
    b = lax.rem(p // 2, B)
    a = p // (2 * B)
    prefix = query_ref.shape[1]
    T, D = state_ref.shape[1], state_ref.shape[2]
    K = cand_ref.shape[1]
    R = K * T
    V = hw.shape[0]

    def dev(a_, b_, c_):
        return (a_ * B + b_) * 2 + c_

    def back(x, d, m):
        return lax.rem(x - d + m, m) if d else x

    peers = nearest(a, A)
    mate = dev(a, b, 1 - c)
    barrier = pltpu.get_barrier_semaphore()
    for z in peers:
        pl.semaphore_signal(barrier, inc=1, device_id=(g, dev(z, b, c)), device_id_type=MESH)
    for e in range(1, B):
        pl.semaphore_signal(
            barrier, inc=1, device_id=(g, dev(a, lax.rem(b + e, B), c)), device_id_type=MESH
        )
    pl.semaphore_signal(barrier, inc=1, device_id=(g, mate), device_id_type=MESH)

    def fetch(src, dst, sem):
        cp = pltpu.make_async_copy(src, dst, sem)
        cp.start()
        return cp

    pc = D // P_CHUNKS
    tiles = [(lo, min(TILE, V - lo)) for lo in range(0, V, TILE)]
    first = [
        fetch(src, dst, in_sem.at[i])
        for i, (src, dst) in enumerate(
            [(state_hbm, state_ref), (ids_hbm, ids_ref), (len_hbm, len_ref)]
        )
    ]
    second = [
        fetch(src, dst, in_sem.at[3 + i])
        for i, (src, dst) in enumerate([(query_hbm, query_ref), (bias_hbm, bias_ref)])
    ]
    pw_copies = [
        fetch(pw_hbm.at[:, pl.ds(i * pc, pc)], pw.at[:, pl.ds(i * pc, pc)], pw_sem.at[i])
        for i in range(P_CHUNKS)
    ]
    third = [
        fetch(src, dst, in_sem.at[5 + i])
        for i, (src, dst) in enumerate([(cand_hbm, cand_ref), (gain_hbm, gain_ref)])
    ]
    for cp in first:
        cp.wait()
    tok = lax.broadcasted_iota(jnp.int32, (T, LANES), 0)
    idv = jnp.zeros((T, LANES), jnp.int32)
    for t in range(T):
        idv = jnp.where(tok == t, ids_ref[0, t], idv)
    lenv = jnp.full((T, LANES), len_ref[0], jnp.int32)
    caps[p, :, 0:D] = state_ref[0]
    meta = jnp.concatenate([idv >> 8, idv & 255, lenv], axis=1)
    caps[p, :, D : D + 3 * LANES] = meta.astype(jnp.float32).astype(jnp.bfloat16)

    pl.semaphore_wait(barrier, (A - 1) + (B - 1) + 1)

    drains = []

    def exchange(buf, start, sent, zr, yr, cr):
        def copy(slot, target, rsem):
            return pltpu.make_async_remote_copy(
                src_ref=buf.at[slot],
                dst_ref=buf.at[slot],
                send_sem=sent,
                recv_sem=rsem,
                device_id=(g, target),
                device_id_type=MESH,
            )

        def send(slot, target, rsem):
            copy(slot, target, rsem).start()

        def to_row(slot, z):
            for e in range(1, B):
                send(slot, dev(a, lax.rem(b + e, B), c), yr.at[z, e - 1])

        def from_row(z):
            for e in range(1, B):
                slot = dev(z, back(b, e, B), c)
                copy(slot, mate, yr.at[z, e - 1]).wait_recv()
                send(slot, mate, cr)

        def from_column(z):
            slot = dev(z, b, c)
            copy(slot, mate, zr.at[z]).wait_recv()
            to_row(slot, z)
            send(slot, mate, cr)

        def finish():
            copy(pl.ds(0, A * B), mate, cr).wait_recv()

        drains.append(lambda: copy(pl.ds(0, A - 1 + A * (B - 1) + A * B), mate, cr).wait_send())
        to_row(p, a)
        for z in peers:
            send(p, dev(z, b, c), zr.at[a])
        send(p, mate, cr)
        steps = [(start + 2.0, lambda: from_row(a))]
        for i, z in enumerate(peers):
            at = start + 1.9 + 0.9 * i
            steps.append((at, functools.partial(from_column, z)))
            steps.append((at + 2.1, functools.partial(from_row, z)))
        steps.append((max(at for at, _ in steps) + 1.0, finish))
        return steps

    def in_order(steps):
        return [step for _, step in sorted(steps, key=lambda item: item[0])]

    def project(i):
        pw_copies[i].wait()
        cols = pl.ds(i * pc, pc)
        summed = jnp.dot(query_ref[0], pw[:, cols], preferred_element_type=jnp.float32)
        kv[0:prefix, cols] = (summed + bias_ref[cols].astype(jnp.float32).reshape(1, pc)).astype(jnp.bfloat16)

    relay = in_order(exchange(caps, 0.0, s1.at[0], z1.at[0], y1.at[0], c1.at[0]))
    for cp in second:
        cp.wait()
    for i in range(P_CHUNKS):
        project(i)
    hw_copies = [
        fetch(hw_hbm.at[pl.ds(lo, width)], hw.at[pl.ds(lo, width)], hw_sem.at[i])
        for i, (lo, width) in enumerate(tiles)
    ]
    for step in relay:
        step()
    for cp in third:
        cp.wait()

    blocks = [caps[cand_ref[0, k]].astype(jnp.float32) for k in range(K)]
    block = jnp.concatenate(blocks, axis=0)
    states = block[:, 0:D]
    codes = block[:, D : D + 2 * LANES].astype(jnp.bfloat16)
    lengths = block[:, D + 2 * LANES : D + 3 * LANES]
    kv_rows = kv.shape[0]
    pad = jnp.zeros((kv_rows - prefix - R, D), jnp.float32)
    kv[prefix:kv_rows, :] = jnp.concatenate([states, pad], axis=0).astype(jnp.bfloat16)

    per = GROUP // HEAD_DIM
    row = lax.broadcasted_iota(jnp.int32, (per * R, kv_rows), 0) % R
    col = lax.broadcasted_iota(jnp.int32, (per * R, kv_rows), 1)
    rel = col - prefix
    allowed = (col < prefix) | (
        (rel >= 0) & (rel < R) & (rel // T == row // T) & (rel % T <= row % T)
    )
    lane_head = lax.broadcasted_iota(jnp.int32, (R, GROUP), 1) // HEAD_DIM
    scores = []
    for i in range(D // GROUP):
        cols = slice(i * GROUP, (i + 1) * GROUP)
        s = states[:, cols]
        q = jnp.concatenate([jnp.where(lane_head == h, s, 0.0) for h in range(per)], axis=0)
        part = lax.dot_general(
            q.astype(jnp.bfloat16),
            kv[:, cols],
            (((1,), (1,)), ((), ())),
            preferred_element_type=jnp.float32,
        )
        scores.append(jnp.where(allowed, part * SCALE, -jnp.inf))
    scores = jnp.concatenate(scores, axis=0)
    expo = jnp.exp(scores - jnp.max(scores, -1, keepdims=True))
    weights = (expo / jnp.sum(expo, -1, keepdims=True)).astype(jnp.bfloat16)
    mixed = []
    for i in range(D // GROUP):
        cols = slice(i * GROUP, (i + 1) * GROUP)
        mix = jnp.dot(
            weights[i * per * R : (i + 1) * per * R],
            kv[:, cols],
            preferred_element_type=jnp.float32,
        )
        total = states[:, cols]
        for h in range(per):
            total = total + jnp.where(lane_head == h, mix[h * R : (h + 1) * R], 0.0)
        mixed.append(total)
    mixed = jnp.concatenate(mixed, axis=1)
    inv = lax.rsqrt(jnp.mean(mixed * mixed, -1, keepdims=True) + EPS)
    hidden = (mixed * inv * gain_ref[...]).astype(jnp.bfloat16)

    spans = feature_spans(D)
    rows = n * R
    code_at = spans[0][1]
    for k, (at, hc) in enumerate(spans):
        hid[k][p, :, 0:hc] = hidden[:, at : at + hc]
    hid[0][p, :, code_at : code_at + 2 * LANES] = codes
    queue, ends = [], []
    for k in range(len(spans)):
        share = exchange(hid[k], PACE * k, s2.at[k], z2.at[k], y2.at[k], c2.at[k])
        queue += share[:-1]
        ends.append(share[-1])
    queue.sort(key=lambda item: item[0])
    for cp in hw_copies:
        cp.wait()
    for k, (at, hc) in enumerate(spans):
        while queue and queue[0][0] < ends[k][0]:
            queue.pop(0)[1]()
        ends[k][1]()
        flat[:, 0:hc] = hid[k][:, :, 0:hc].reshape(rows, hc)
        last = k + 1 == len(spans)
        if last:
            ids = hid[0][:, :, code_at : code_at + 2 * LANES].astype(jnp.float32).reshape(rows, 2 * LANES)
            ids = (ids[:, 0:LANES] * 256.0 + ids[:, LANES : 2 * LANES]).T[0:1]
            want = ids.astype(jnp.int32) - p * V
            top = jnp.full((1, rows), -jnp.inf, jnp.float32)
            picked = jnp.zeros((1, rows), jnp.float32)
        for lo, width in tiles:
            part = lax.dot_general(
                hw[lo : lo + width, at : at + hc],
                flat[:, 0:hc],
                (((1,), (1,)), ((), ())),
                preferred_element_type=jnp.float32,
            )
            if k:
                part = part + logit[lo : lo + width]
            logit[lo : lo + width] = part
            if last:
                top = jnp.maximum(top, jnp.max(part, 0, keepdims=True))
                here = lax.broadcasted_iota(jnp.int32, (width, rows), 0) + lo
                picked = picked + jnp.sum(jnp.where(here == want, part, 0.0), 0, keepdims=True)
    total = jnp.zeros((1, rows), jnp.float32)
    for lo, width in tiles:
        total = total + jnp.sum(jnp.exp(logit[lo : lo + width] - top), 0, keepdims=True)
    st_in[p] = jnp.concatenate([top + jnp.log(total), picked], axis=0)

    def stat_copy(q, slots):
        return pltpu.make_async_remote_copy(
            src_ref=st_in.at[slots],
            dst_ref=st_in.at[slots],
            send_sem=ss3.at[0],
            recv_sem=sr3.at[0],
            device_id=(g, q),
            device_id_type=MESH,
        )

    for i in range(1, n):
        stat_copy(lax.rem(p + i, n), p).start()
    everyone = stat_copy(mate, pl.ds(0, n - 1))
    everyone.wait_recv()

    every_stat = st_in[...]
    lses = every_stat[:, 0:1, :]
    top = jnp.max(lses, axis=0)
    total = jnp.sum(jnp.exp(lses - top[None]), axis=0)
    picked = jnp.sum(every_stat[:, 1:2, :], axis=0)
    loglik = picked - (top + jnp.log(total))
    mine = lax.broadcasted_iota(jnp.int32, (R, rows), 1) == (
        lax.broadcasted_iota(jnp.int32, (R, rows), 0) + p * R
    )
    loglik = jnp.sum(jnp.where(mine, loglik, 0.0), -1, keepdims=True)
    row = lax.broadcasted_iota(jnp.int32, (R, LANES), 0) % T
    lane = lax.broadcasted_iota(jnp.int32, (R, LANES), 1)
    value = jnp.where(row.astype(jnp.float32) < lengths, loglik, 0.0)
    value = jnp.where(lane == row, value, 0.0)
    for k in range(K):
        line = jnp.sum(value[k * T : (k + 1) * T], axis=0, keepdims=True)
        out_ref[0, k : k + 1, :] = line[:, 0:T]
    everyone.wait_send()
    for drain in drains:
        drain()


def local(n, rows_b, query, pw, bias, cand, states, ids, lens, gain, hw):
    T, D = states.shape[1:]
    K = cand.shape[1]
    R = K * T
    V = hw.shape[1]
    W_CHUNKS = pl.cdiv(V, TILE)
    A, B = n // (2 * rows_b), rows_b
    dma = pltpu.SemaphoreType.DMA
    vmem = pl.BlockSpec(memory_space=pltpu.VMEM)
    hbm = pl.BlockSpec(memory_space=pl.ANY)
    spans = feature_spans(D)

    def gather(chunks):
        shapes = [(chunks,), (chunks, A), (chunks, A, B - 1), (chunks,)]
        return [dma(shape) for shape in shapes]

    return pl.pallas_call(
        functools.partial(kernel, n, rows_b),
        out_shape=jax.ShapeDtypeStruct((1, K, T), jnp.float32),
        in_specs=[hbm] * 9,
        out_specs=vmem,
        scratch_shapes=[
            pltpu.VMEM(query.shape, jnp.bfloat16),
            pltpu.VMEM(bias.shape, jnp.bfloat16),
            pltpu.SMEM(cand.shape, jnp.int32),
            pltpu.VMEM(states.shape, jnp.bfloat16),
            pltpu.SMEM(ids.shape, jnp.int32),
            pltpu.SMEM(lens.shape, jnp.int32),
            pltpu.VMEM((1, D), jnp.float32),
            dma((7,)),
            pltpu.VMEM(pw.shape, jnp.bfloat16),
            pltpu.VMEM((V, D), jnp.bfloat16),
            pltpu.VMEM((n, T, D + 3 * LANES), jnp.bfloat16),
            pltpu.VMEM((48, D), jnp.bfloat16),
            [
                pltpu.VMEM((n, R, hc if k else hc + 2 * LANES), jnp.bfloat16)
                for k, (_, hc) in enumerate(spans)
            ],
            pltpu.VMEM((n * R, max(hc for _, hc in spans)), jnp.bfloat16),
            pltpu.VMEM((V, n * R), jnp.float32),
            pltpu.VMEM((n, 2, n * R), jnp.float32),
            dma((P_CHUNKS,)),
            dma((W_CHUNKS,)),
            *gather(1),
            *gather(len(spans)),
            dma((1,)),
            dma((1,)),
        ],
        compiler_params=pltpu.CompilerParams(
            collective_id=0, has_side_effects=True, vmem_limit_bytes=60000 * 1024
        ),
        name="rerank",
    )(query, pw, bias, cand, states, ids, lens, gain.reshape(1, D), hw.T)


def solution(mesh):
    n = mesh.shape["dp"]
    rows_b = 1 << (((n // 2).bit_length() - 1) // 2)
    in_specs = (
        P(("groups", "dp"), None, None),
        P(),
        P(),
        P(("groups", "dp"), None),
        P(("groups", "dp"), None, None),
        P(("groups", "dp"), None),
        P(("groups", "dp")),
        P(),
        P(None, "dp"),
    )
    return jax.shard_map(
        functools.partial(local, n, rows_b),
        mesh=mesh,
        in_specs=in_specs,
        out_specs=P(("groups", "dp"), None, None),
        check_vma=False,
    )
```

```python
import functools

import jax
import jax.numpy as jnp
from jax import lax
from jax.experimental import pallas as pl
from jax.experimental.pallas import tpu as pltpu
from jax.sharding import PartitionSpec as P

HEAD_DIM = 64
SCALE = 0.015625
EPS = 1e-06
LANES = 128
GROUP = 256
MESH = pl.DeviceIdType.MESH
P_CHUNKS = 4
H_SPLIT = (1, 1, 1, 1)
C_SPLIT = (1,)
TILE = 256
PACE = 1.0
C_PACE = 1.2
FINISH = 2.2


def ring_order(count):
    return sorted(range(1, count), key=lambda d: (min(d, count - d), d))


def nearest(a, count):
    if count != 4:
        return [lax.rem(a + d, count) for d in ring_order(count)]
    high = a // 2
    low = 1 - high
    near = high * (3 - a) + low * a
    return [high * (3 - q) + low * q for q in (1 - near, 2, 3)]


def feature_spans(width, split):
    unit, at, spans = width // sum(split), 0, []
    for share in split:
        spans.append((at, share * unit))
        at += share * unit
    return spans


def kernel(
    n,
    rows_b,
    query_hbm,
    pw_hbm,
    bias_hbm,
    cand_hbm,
    state_hbm,
    ids_hbm,
    len_hbm,
    gain_hbm,
    hw_hbm,
    out_ref,
    query_ref,
    bias_ref,
    cand_ref,
    state_ref,
    ids_ref,
    len_ref,
    gain_ref,
    in_sem,
    pw,
    hw,
    caps,
    kv,
    hid,
    flat,
    logit,
    st_in,
    pw_sem,
    hw_sem,
    s1,
    z1,
    y1,
    c1,
    s2,
    z2,
    y2,
    c2,
    ss3,
    sr3,
):
    B = rows_b
    A = n // (2 * B)
    g = lax.axis_index("groups")
    p = lax.axis_index("dp")
    c = lax.rem(p, 2)
    b = lax.rem(p // 2, B)
    a = p // (2 * B)
    prefix = query_ref.shape[1]
    T, D = state_ref.shape[1], state_ref.shape[2]
    K = cand_ref.shape[1]
    R = K * T
    V = hw.shape[0]

    def dev(a_, b_, c_):
        return (a_ * B + b_) * 2 + c_

    def back(x, d, m):
        return lax.rem(x - d + m, m) if d else x

    peers = nearest(a, A)
    mate = dev(a, b, 1 - c)
    barrier = pltpu.get_barrier_semaphore()
    for z in peers:
        pl.semaphore_signal(barrier, inc=1, device_id=(g, dev(z, b, c)), device_id_type=MESH)
    for e in range(1, B):
        pl.semaphore_signal(
            barrier, inc=1, device_id=(g, dev(a, lax.rem(b + e, B), c)), device_id_type=MESH
        )
    pl.semaphore_signal(barrier, inc=1, device_id=(g, mate), device_id_type=MESH)

    def fetch(src, dst, sem):
        cp = pltpu.make_async_copy(src, dst, sem)
        cp.start()
        return cp

    pc = D // P_CHUNKS
    tiles = [(lo, min(TILE, V - lo)) for lo in range(0, V, TILE)]
    first = [
        fetch(src, dst, in_sem.at[i])
        for i, (src, dst) in enumerate(
            [(state_hbm, state_ref), (ids_hbm, ids_ref), (len_hbm, len_ref)]
        )
    ]
    second = [
        fetch(src, dst, in_sem.at[3 + i])
        for i, (src, dst) in enumerate([(query_hbm, query_ref), (bias_hbm, bias_ref)])
    ]
    pw_copies = [
        fetch(pw_hbm.at[:, pl.ds(i * pc, pc)], pw.at[:, pl.ds(i * pc, pc)], pw_sem.at[i])
        for i in range(P_CHUNKS)
    ]
    third = [
        fetch(src, dst, in_sem.at[5 + i])
        for i, (src, dst) in enumerate([(cand_hbm, cand_ref), (gain_hbm, gain_ref)])
    ]
    for cp in first:
        cp.wait()
    tok = lax.broadcasted_iota(jnp.int32, (T, LANES), 0)
    lane = lax.broadcasted_iota(jnp.int32, (T, LANES), 1)
    idv = jnp.zeros((T, LANES), jnp.int32)
    for t in range(T):
        idv = jnp.where(tok == t, ids_ref[0, t], idv)
    meta = jnp.where(lane == 0, idv >> 8, jnp.where(lane == 1, idv & 255, len_ref[0, 0]))
    cap_spans = feature_spans(D, C_SPLIT)
    meta_at = cap_spans[0][1]
    for k, (at, hc) in enumerate(cap_spans):
        caps[k][p, :, 0:hc] = state_ref[0, :, at : at + hc]
    caps[0][p, :, meta_at : meta_at + LANES] = meta.astype(jnp.float32).astype(jnp.bfloat16)

    pl.semaphore_wait(barrier, (A - 1) + (B - 1) + 1)

    drains = []

    def exchange(buf, start, sent, zr, yr, cr):
        def copy(slot, target, rsem):
            return pltpu.make_async_remote_copy(
                src_ref=buf.at[slot],
                dst_ref=buf.at[slot],
                send_sem=sent,
                recv_sem=rsem,
                device_id=(g, target),
                device_id_type=MESH,
            )

        def send(slot, target, rsem):
            copy(slot, target, rsem).start()

        def to_row(slot, z):
            for e in range(1, B):
                send(slot, dev(a, lax.rem(b + e, B), c), yr.at[z, e - 1])

        def from_row(z):
            for e in range(1, B):
                slot = dev(z, back(b, e, B), c)
                copy(slot, mate, yr.at[z, e - 1]).wait_recv()
                send(slot, mate, cr)

        def from_column(z):
            slot = dev(z, b, c)
            copy(slot, mate, zr.at[z]).wait_recv()
            to_row(slot, z)
            send(slot, mate, cr)

        def finish():
            copy(pl.ds(0, A * B), mate, cr).wait_recv()

        drains.append(lambda: copy(pl.ds(0, A - 1 + A * (B - 1) + A * B), mate, cr).wait_send())
        to_row(p, a)
        for z in peers:
            send(p, dev(z, b, c), zr.at[a])
        send(p, mate, cr)
        steps = [(start + 2.0, lambda: from_row(a))]
        for i, z in enumerate(peers):
            at = start + 1.9 + 0.9 * i
            steps.append((at, functools.partial(from_column, z)))
            steps.append((at + 2.1, functools.partial(from_row, z)))
        steps.append((max(at for at, _ in steps) + FINISH, finish))
        return steps

    def in_order(steps):
        return [step for _, step in sorted(steps, key=lambda item: item[0])]

    def project(i):
        pw_copies[i].wait()
        cols = pl.ds(i * pc, pc)
        summed = jnp.dot(query_ref[0], pw[:, cols], preferred_element_type=jnp.float32)
        kv[0:prefix, cols] = (summed + bias_ref[cols].astype(jnp.float32).reshape(1, pc)).astype(jnp.bfloat16)

    relay = []
    for k in range(len(cap_spans)):
        relay += exchange(caps[k], C_PACE * k, s1.at[k], z1.at[k], y1.at[k], c1.at[k])
    relay = in_order(relay)
    for cp in second:
        cp.wait()
    for i in range(P_CHUNKS):
        project(i)
    hw_copies = [
        fetch(hw_hbm.at[pl.ds(lo, width)], hw.at[pl.ds(lo, width)], hw_sem.at[i])
        for i, (lo, width) in enumerate(tiles)
    ]
    for step in relay:
        step()
    for cp in third:
        cp.wait()

    picks = [cand_ref[0, k] for k in range(K)]

    def chosen(k):
        return jnp.concatenate([caps[k][pick].astype(jnp.float32) for pick in picks], axis=0)

    parts = [chosen(k) for k in range(len(cap_spans))]
    states = jnp.concatenate([part[:, 0:hc] for part, (_, hc) in zip(parts, cap_spans)], axis=1)
    metas = parts[0][:, meta_at : meta_at + LANES]
    codes = metas.astype(jnp.bfloat16)
    lengths = metas[:, 2:3]
    kv_rows = kv.shape[0]
    pad = jnp.zeros((kv_rows - prefix - R, D), jnp.float32)
    kv[prefix:kv_rows, :] = jnp.concatenate([states, pad], axis=0).astype(jnp.bfloat16)

    per = GROUP // HEAD_DIM
    row = lax.broadcasted_iota(jnp.int32, (per * R, kv_rows), 0) % R
    col = lax.broadcasted_iota(jnp.int32, (per * R, kv_rows), 1)
    rel = col - prefix
    allowed = (col < prefix) | (
        (rel >= 0) & (rel < R) & (rel // T == row // T) & (rel % T <= row % T)
    )
    lane_head = lax.broadcasted_iota(jnp.int32, (R, GROUP), 1) // HEAD_DIM
    scores = []
    for i in range(D // GROUP):
        cols = slice(i * GROUP, (i + 1) * GROUP)
        s = states[:, cols]
        q = jnp.concatenate([jnp.where(lane_head == h, s, 0.0) for h in range(per)], axis=0)
        part = lax.dot_general(
            q.astype(jnp.bfloat16),
            kv[:, cols],
            (((1,), (1,)), ((), ())),
            preferred_element_type=jnp.float32,
        )
        scores.append(jnp.where(allowed, part * SCALE, -jnp.inf))
    scores = jnp.concatenate(scores, axis=0)
    expo = jnp.exp(scores - jnp.max(scores, -1, keepdims=True))
    weights = (expo / jnp.sum(expo, -1, keepdims=True)).astype(jnp.bfloat16)
    mixed = []
    for i in range(D // GROUP):
        cols = slice(i * GROUP, (i + 1) * GROUP)
        mix = jnp.dot(
            weights[i * per * R : (i + 1) * per * R],
            kv[:, cols],
            preferred_element_type=jnp.float32,
        )
        total = states[:, cols]
        for h in range(per):
            total = total + jnp.where(lane_head == h, mix[h * R : (h + 1) * R], 0.0)
        mixed.append(total)
    mixed = jnp.concatenate(mixed, axis=1)
    inv = lax.rsqrt(jnp.mean(mixed * mixed, -1, keepdims=True) + EPS)
    hidden = (mixed * inv * gain_ref[...]).astype(jnp.bfloat16)

    spans = feature_spans(D, H_SPLIT)
    rows = n * R
    code_at = spans[0][1]
    for k, (at, hc) in enumerate(spans):
        hid[k][p, :, 0:hc] = hidden[:, at : at + hc]
    hid[0][p, :, code_at : code_at + LANES] = codes
    queue, ends = [], []
    for k in range(len(spans)):
        share = exchange(hid[k], PACE * k, s2.at[k], z2.at[k], y2.at[k], c2.at[k])
        queue += share[:-1]
        ends.append(share[-1])
    queue.sort(key=lambda item: item[0])
    for cp in hw_copies:
        cp.wait()
    for k, (at, hc) in enumerate(spans):
        while queue and queue[0][0] < ends[k][0]:
            queue.pop(0)[1]()
        ends[k][1]()
        flat[:, 0:hc] = hid[k][:, :, 0:hc].reshape(rows, hc)
        last = k + 1 == len(spans)
        if last:
            ids = hid[0][:, :, code_at : code_at + LANES].astype(jnp.float32).reshape(rows, LANES)
            ids = jnp.broadcast_to(ids[:, 0:1] * 256.0 + ids[:, 1:2], (rows, LANES)).T[0:1]
            want = ids.astype(jnp.int32) - p * V
            top = jnp.full((1, rows), -jnp.inf, jnp.float32)
            picked = jnp.zeros((1, rows), jnp.float32)
        for lo, width in tiles:
            part = lax.dot_general(
                hw[lo : lo + width, at : at + hc],
                flat[:, 0:hc],
                (((1,), (1,)), ((), ())),
                preferred_element_type=jnp.float32,
            )
            if k:
                part = part + logit[lo : lo + width]
            logit[lo : lo + width] = part
            if last:
                top = jnp.maximum(top, jnp.max(part, 0, keepdims=True))
                here = lax.broadcasted_iota(jnp.int32, (width, rows), 0) + lo
                picked = picked + jnp.sum(jnp.where(here == want, part, 0.0), 0, keepdims=True)
    total = jnp.zeros((1, rows), jnp.float32)
    for lo, width in tiles:
        total = total + jnp.sum(jnp.exp(logit[lo : lo + width] - top), 0, keepdims=True)
    st_in[p] = jnp.concatenate([top + jnp.log(total), picked], axis=0)

    def stat_copy(q, slots):
        return pltpu.make_async_remote_copy(
            src_ref=st_in.at[slots],
            dst_ref=st_in.at[slots],
            send_sem=ss3.at[0],
            recv_sem=sr3.at[0],
            device_id=(g, q),
            device_id_type=MESH,
        )

    for i in range(1, n):
        stat_copy(lax.rem(p + i, n), p).start()
    everyone = stat_copy(mate, pl.ds(0, n - 1))
    everyone.wait_recv()

    every_stat = st_in[...]
    lses = every_stat[:, 0:1, :]
    top = jnp.max(lses, axis=0)
    total = jnp.sum(jnp.exp(lses - top[None]), axis=0)
    picked = jnp.sum(every_stat[:, 1:2, :], axis=0)
    loglik = picked - (top + jnp.log(total))
    mine = lax.broadcasted_iota(jnp.int32, (R, rows), 1) == (
        lax.broadcasted_iota(jnp.int32, (R, rows), 0) + p * R
    )
    loglik = jnp.sum(jnp.where(mine, loglik, 0.0), -1, keepdims=True)
    row = lax.broadcasted_iota(jnp.int32, (R, LANES), 0) % T
    lane = lax.broadcasted_iota(jnp.int32, (R, LANES), 1)
    value = jnp.where(row.astype(jnp.float32) < lengths, loglik, 0.0)
    value = jnp.where(lane == row, value, 0.0)
    for k in range(K):
        line = jnp.sum(value[k * T : (k + 1) * T], axis=0, keepdims=True)
        out_ref[0, k : k + 1, :] = line[:, 0:T]
    everyone.wait_send()
    for drain in drains:
        drain()


def local(n, rows_b, query, pw, bias, cand, states, ids, lens, gain, hw):
    T, D = states.shape[1:]
    K = cand.shape[1]
    R = K * T
    V = hw.shape[1]
    W_CHUNKS = pl.cdiv(V, TILE)
    A, B = n // (2 * rows_b), rows_b
    dma = pltpu.SemaphoreType.DMA
    vmem = pl.BlockSpec(memory_space=pltpu.VMEM)
    hbm = pl.BlockSpec(memory_space=pl.ANY)
    spans = feature_spans(D, H_SPLIT)

    def gather(chunks):
        shapes = [(chunks,), (chunks, A), (chunks, A, B - 1), (chunks,)]
        return [dma(shape) for shape in shapes]

    return pl.pallas_call(
        functools.partial(kernel, n, rows_b),
        out_shape=pltpu.VMEM((1, K, T), jnp.float32),
        in_specs=[hbm] * 9,
        out_specs=vmem,
        scratch_shapes=[
            pltpu.VMEM(query.shape, jnp.bfloat16),
            pltpu.VMEM(bias.shape, jnp.bfloat16),
            pltpu.SMEM(cand.shape, jnp.int32),
            pltpu.VMEM(states.shape, jnp.bfloat16),
            pltpu.SMEM(ids.shape, jnp.int32),
            pltpu.SMEM((1, 1), jnp.int32),
            pltpu.VMEM((1, D), jnp.float32),
            dma((7,)),
            pltpu.VMEM(pw.shape, jnp.bfloat16),
            pltpu.VMEM((V, D), jnp.bfloat16),
            [
                pltpu.VMEM((n, T, hc if k else hc + LANES), jnp.bfloat16)
                for k, (_, hc) in enumerate(feature_spans(D, C_SPLIT))
            ],
            pltpu.VMEM((48, D), jnp.bfloat16),
            [
                pltpu.VMEM((n, R, hc if k else hc + LANES), jnp.bfloat16)
                for k, (_, hc) in enumerate(spans)
            ],
            pltpu.VMEM((n * R, max(hc for _, hc in spans)), jnp.bfloat16),
            pltpu.VMEM((V, n * R), jnp.float32),
            pltpu.VMEM((n, 2, n * R), jnp.float32),
            dma((P_CHUNKS,)),
            dma((W_CHUNKS,)),
            *gather(len(C_SPLIT)),
            *gather(len(spans)),
            dma((1,)),
            dma((1,)),
        ],
        compiler_params=pltpu.CompilerParams(
            collective_id=0, has_side_effects=True, vmem_limit_bytes=60000 * 1024
        ),
        name="rerank",
    )(query, pw, bias, cand, states, ids, lens.reshape(1, 1), gain.reshape(1, D), hw.T)


def solution(mesh):
    n = mesh.shape["dp"]
    rows_b = 1 << (((n // 2).bit_length() - 1) // 2)
    in_specs = (
        P(("groups", "dp"), None, None),
        P(),
        P(),
        P(("groups", "dp"), None),
        P(("groups", "dp"), None, None),
        P(("groups", "dp"), None),
        P(("groups", "dp")),
        P(),
        P(None, "dp"),
    )
    return jax.shard_map(
        functools.partial(local, n, rows_b),
        mesh=mesh,
        in_specs=in_specs,
        out_specs=P(("groups", "dp"), None, None),
        check_vma=False,
    )
```
